512 devices in a mesh: dp: 4 (over z_hi), loop: 128 (over x, y, z_lo, core).
Axes of the slice: x: 4, y: 8, z: 8 (z_hi: 4, z_lo: 2; z = z_hi * 2 + z_lo), core: 2. Of those that a mesh axis runs over, the one named last changes fastest.
Arguments:
- tokens: bfloat16 [8192, 2048], P('loop', 'dp'), may hold values from -6 to 6
- cotangent: bfloat16 [8192, 2048], P('loop', 'dp'), may hold values from -6 to 6
- up_first: bfloat16 [128, 256, 128], P('loop'), may hold values from -0.5 to 0.5
- up_second: bfloat16 [256, 128, 128], P('loop'), may hold values from -0.5 to 0.5
- down_first: bfloat16 [256, 128, 128], P('loop'), may hold values from -0.5 to 0.5
- down_second: bfloat16 [128, 256, 128], P('loop'), may hold values from -0.25 to 0.25
- perm_up: int32 [128], replicated, may hold values from 0 to 127, each once
- perm_down: int32 [128], replicated, may hold values from 0 to 127, each once
Outputs:
- mixed: bfloat16 [8192, 2048], P('loop', 'dp')
- grad_tokens: bfloat16 [8192, 2048], P('loop', 'dp')
- grad_up_first: float32 [128, 256, 128], P('loop')
- grad_up_second: float32 [256, 128, 128], P('loop')
- grad_down_first: float32 [256, 128, 128], P('loop')
- grad_down_second: float32 [128, 256, 128], P('loop')
The draws below stay inside these ranges and needn't reach their ends.
Inputs may be any that keep to these rules, and one draw needn't show every extreme that they name: perm_up holds each of 0 to 127 once. perm_down holds each of 0 to 127 once.
All inputs are finite; a program needn't handle non-finite values.
Results may differ from the reference program's by a relative error of at most 0.01.
Values may be sent and summed in bfloat16 or wider, within the bound.
A program may use at most 64 MiB of HBM per device.

```python
import math
import jax
import jax.numpy as jnp
from jax import lax

D = 8192
BLK = 128
TOKENS = 2048
BD = 256
GRP = 2
PB = 1
N_LOOP = 128


def levels(rng, dims, shards, least, largest):
    level = 1.0
    for axis_at, parts in shards:
        steps = jax.random.uniform(jax.random.fold_in(jax.random.fold_in(rng, 6), axis_at), (parts,), jnp.float32, least / len(shards), largest / len(shards))
        level = level * jnp.repeat(jnp.exp(steps), dims[axis_at] // parts).reshape((-1,) + (1,) * (len(dims) - 1 - axis_at))
    return level


def gaussian(own_key, extent, scale, limit, shards=(), held_as=jnp.bfloat16):
    loudness = levels(own_key, extent, shards, -0.22, 0.18) if shards else 1.0
    entries = jax.random.normal(own_key, extent, jnp.float32) * scale * loudness
    return jnp.minimum(jnp.maximum(entries, -limit), limit).astype(held_as)


def setup_inputs(seed: int = 0) -> dict:
    splits = jax.random.split(jax.random.key(seed), 9)
    return {
        "tokens": gaussian(splits[0], (D, TOKENS), 1.0, 6.0, ((0, 128), (1, 4))),
        "cotangent": gaussian(splits[1], (D, TOKENS), 1.0, 6.0, ((0, 128), (1, 4))),
        "up_first": gaussian(splits[2], (BLK, BD, BLK), BLK ** -0.5, 0.5, ((0, 128),)),
        "up_second": gaussian(splits[3], (BD, BLK, BLK), BLK ** -0.5, 0.5, ((0, 128),)),
        "down_first": gaussian(splits[4], (BD, BLK, BLK), BLK ** -0.5, 0.5, ((0, 128),)),
        "down_second": gaussian(splits[5], (BLK, BD, BLK), (GRP * BD) ** -0.5, 0.25, ((0, 128),)),
        "perm_up": jax.random.permutation(splits[6], BLK).astype(jnp.int32),
        "perm_down": jax.random.permutation(splits[7], BLK).astype(jnp.int32),
    }


def gelu_parts(pre_act):
    cumul = 0.5 * (1.0 + jax.scipy.special.erf(pre_act * (1.0 / math.sqrt(2.0))))
    slope = cumul + pre_act * jnp.exp(-0.5 * pre_act * pre_act) * (1.0 / math.sqrt(2.0 * math.pi))
    return (pre_act * cumul, slope)

def inverse_of(permute):
    return jnp.zeros(permute.shape, jnp.int32).at[permute].set(jnp.arange(permute.shape[0], dtype=jnp.int32))

def to_blocks(field):
    width = field.shape[1]
    shaped = field.reshape(N_LOOP // 2, 2, PB, BLK // 2, width).transpose(0, 2, 1, 3, 4)
    return shaped.reshape(D // BLK, BLK, width)

def from_blocks(field):
    width = field.shape[2]
    shaped = field.reshape(N_LOOP // 2, PB, 2, BLK // 2, width).transpose(0, 2, 1, 3, 4)
    return shaped.reshape(D, width)

def reference(tokens, cotangent, up_first, up_second, down_first, down_second, perm_up, perm_down):
    wide = jnp.float32
    narrow = jnp.bfloat16
    blocks = D // BLK
    width = min(1024, TOKENS)
    pieces_count = TOKENS // width
    first_up = up_first.astype(wide).reshape(blocks, GRP, BD, BLK)
    second_up = up_second.astype(wide)
    first_down = down_first.astype(wide)
    last_down = down_second.astype(wide).reshape(blocks, GRP, BD, BLK)
    inverse_up = inverse_of(perm_up)
    inverse_down = inverse_of(perm_down)

    def one_block(carry, pieces):
        x_block, d_block = pieces
        x_wide = to_blocks(x_block.astype(wide))
        d_wide = to_blocks(d_block.astype(wide))
        hidden_one = jnp.einsum('egbi,eit->egbt', first_up, x_wide).reshape(BLK, BD, width).astype(narrow)
        permuted = jnp.take(hidden_one, perm_up, axis=0)
        pre_act = jnp.einsum('boa,abt->bot', second_up, permuted.astype(wide))
        gelu_val, slope = gelu_parts(pre_act)
        activated = gelu_val.astype(narrow)
        mixed_cols = jnp.einsum('bpo,bot->pbt', first_down, activated.astype(wide)).astype(narrow)
        back_rows = jnp.take(mixed_cols, perm_down, axis=0)
        rows_wide = back_rows.astype(wide).reshape(blocks, GRP, BD, width)
        branch_out = from_blocks(jnp.einsum('egbo,egbt->eot', last_down, rows_wide))
        mixed = (x_block.astype(wide) + branch_out).astype(narrow)
        grad_rows = jnp.einsum('egbo,eot->egbt', last_down, d_wide).reshape(BLK, BD, width).astype(narrow)
        g_down_second = jnp.einsum('egbt,eot->egbo', rows_wide, d_wide).reshape(BLK, BD, BLK)
        grad_mixed = jnp.take(grad_rows, inverse_down, axis=0).astype(wide)
        grad_act = jnp.einsum('bpo,pbt->bot', first_down, grad_mixed)
        g_down_first = jnp.einsum('pbt,bot->bpo', grad_mixed, activated.astype(wide))
        grad_pre = (grad_act * slope).astype(narrow).astype(wide)
        g_up_second = jnp.einsum('bot,abt->boa', grad_pre, permuted.astype(wide))
        grad_perm = jnp.einsum('boa,bot->abt', second_up, grad_pre).astype(narrow)
        grad_hidden = jnp.take(grad_perm, inverse_up, axis=0).astype(wide).reshape(blocks, GRP, BD, width)
        g_up_first = jnp.einsum('egbt,eit->egbi', grad_hidden, x_wide).reshape(BLK, BD, BLK)
        grad_branch = from_blocks(jnp.einsum('egbi,egbt->eit', first_up, grad_hidden))
        grad_tokens = (d_block.astype(wide) + grad_branch).astype(narrow)
        carry = (carry[0] + g_up_first, carry[1] + g_up_second, carry[2] + g_down_first, carry[3] + g_down_second)
        return (carry, (mixed, grad_tokens))
    start = (jnp.zeros((BLK, BD, BLK), wide), jnp.zeros((BD, BLK, BLK), wide), jnp.zeros((BD, BLK, BLK), wide), jnp.zeros((BLK, BD, BLK), wide))
    x_stack = tokens.reshape(D, pieces_count, width).transpose(1, 0, 2)
    d_stack = cotangent.reshape(D, pieces_count, width).transpose(1, 0, 2)
    totals, outputs = lax.scan(one_block, start, (x_stack, d_stack))
    scale = 1.0 / math.sqrt(TOKENS)
    mixed = outputs[0].transpose(1, 0, 2).reshape(D, TOKENS)
    grad_tokens = outputs[1].transpose(1, 0, 2).reshape(D, TOKENS)
    return (mixed, grad_tokens, totals[0] * scale, totals[1] * scale, totals[2] * scale, totals[3] * scale)
```

```python
import functools
import math

import jax
import jax.numpy as jnp
from jax import lax
from jax.experimental import pallas as pl
from jax.experimental.pallas import tpu as pltpu
from jax.sharding import PartitionSpec as P

MESH = pl.DeviceIdType.MESH
WIDE = jnp.float32
NARROW = jnp.bfloat16
NX = 4
NY = 8
NZC = 4
N = NX * NY * NZC


def dot(a, b, ca, cb):
    return lax.dot_general(a, b, (((ca,), (cb,)), ((), ())), preferred_element_type=WIDE)


def gelu_parts(pre_act):
    cumul = 0.5 * (1.0 + lax.erf(pre_act * (1.0 / math.sqrt(2.0))))
    slope = cumul + pre_act * jnp.exp(-0.5 * pre_act * pre_act) * (1.0 / math.sqrt(2.0 * math.pi))
    return (pre_act * cumul, slope)


def exchange(
    x_ref, d_ref, uf_ref, us_ref, df_ref, ds_ref, pu_ref, pd_ref,
    mixed_ref, gtok_ref, grads_ref,
    xb, db, sent, got, act, slope, halves, halves_out, halves_in, part, pieces, total, every,
    near_sem, far_sem, pair_send, pair_recv, send_sem, recv_sem, half_send, half_recv,
    scat_send, scat_recv, gath_send, gath_recv,
):
    me = lax.axis_index("loop")
    dp = lax.axis_index("dp")
    n_dp = lax.axis_size("dp")
    core = lax.rem(me, 2)
    zc = lax.rem(me, NZC)
    z = lax.div(zc, 2)
    y = lax.rem(lax.div(me, NZC), NY)
    x = lax.div(me, NZC * NY)
    half = x_ref.shape[0]
    tok = x_ref.shape[1]
    rows = 2 * N

    def moved(dx, dy, dz, dc):
        return (
            (lax.rem(x + dx, NX) * NY + lax.rem(y + dy, NY)) * NZC
            + lax.rem(z + dz, 2) * 2
            + lax.rem(core + dc, 2)
        )

    partner = moved(0, 0, 0, 1)
    along_y = [moved(0, k, 0, 0) for k in range(1, NY)]
    along_x = [moved(k, 0, 0, 0) for k in range(1, NX)]
    along_z = [moved(0, 0, 0, 1), moved(0, 0, 1, 0), moved(0, 0, 1, 1)]

    def signal(sem, who, group):
        pl.semaphore_signal(sem, 1, device_id=(group, who), device_id_type=MESH)

    barrier = pltpu.get_barrier_semaphore()
    for who in along_y + along_x + along_z:
        signal(barrier, who, dp)
    for k in range(1, n_dp):
        signal(barrier, me, lax.rem(dp + k, n_dp))

    down = lax.broadcasted_iota(jnp.int32, (N, N), 0)
    row_up = (down == pu_ref[...]).astype(NARROW)
    row_down = (down == pd_ref[...]).astype(NARROW)
    lane = lax.broadcasted_iota(jnp.int32, (N, rows), 1)
    sub = lax.broadcasted_iota(jnp.int32, (N, rows), 0)
    spread = [(lane == 2 * sub + b).astype(NARROW) for b in range(2)]
    pick_up = [dot(row_up, e, 0, 0).astype(NARROW) for e in spread]
    pick_down = [dot(row_down, e, 1, 0).astype(NARROW) for e in spread]
    w_up = jnp.concatenate([dot(us_ref[b], pick_up[b], 1, 0).astype(NARROW) for b in range(2)], 0)
    w_down = jnp.concatenate(
        [dot(pick_down[b], df_ref[b], 0, 0).astype(NARROW) for b in range(2)], 1
    )

    xb[core] = x_ref[...]
    db[core] = d_ref[...]
    pl.semaphore_wait(barrier, NY - 1 + NX - 1 + 3 + n_dp - 1)

    to_pair = []
    for i, (src, dst) in enumerate(((x_ref, xb), (d_ref, db))):
        copy = pltpu.make_async_remote_copy(
            src, dst.at[core], pair_send.at[i], pair_recv.at[i],
            device_id=(dp, partner), device_id_type=MESH,
        )
        copy.start()
        to_pair.append(copy)
    for who in along_x:
        signal(near_sem, who, dp)

    def send(i, first, last):
        def one(k, carry):
            dzc = lax.div(k, NX * NY)
            rest = lax.rem(k, NX * NY)
            who = moved(lax.div(rest, NY), lax.rem(rest, NY), lax.div(dzc, 2), lax.rem(dzc, 2))
            pltpu.make_async_remote_copy(
                sent.at[i, who], got.at[i, me], send_sem.at[i], recv_sem.at[i],
                device_id=(dp, who), device_id_type=MESH,
            ).start()
            return carry

        lax.fori_loop(first, last, one, 0)

    def all_of(i, sem):
        return pltpu.make_async_copy(sent.at[i, pl.ds(0, N - 1)], got.at[i, pl.ds(0, N - 1)], sem.at[i])

    def put(i, value):
        sent[i] = value.astype(NARROW).reshape(N, 2, tok)
        got[i, me] = sent[i, me]

    def taken(i):
        all_of(i, recv_sem).wait()
        return got[i].reshape(rows, tok)

    to_pair[0].wait_recv()
    x_block = xb[...].reshape(2 * half, tok)
    put(0, dot(uf_ref[...], x_block, 1, 0))
    pl.semaphore_wait(near_sem, NX - 1)
    for who in along_z:
        signal(far_sem, who, dp)
    send(0, 1, NX * NY)
    to_pair[1].wait_recv()
    d_block = db[...].reshape(2 * half, tok)
    put(1, dot(ds_ref[...], d_block, 1, 0))
    pl.semaphore_wait(far_sem, 3)
    send(0, NX * NY, N)
    send(1, 1, N)

    permuted = taken(0)
    gelu_val, slope_val = gelu_parts(dot(w_up, permuted, 1, 0))
    act[...] = gelu_val.astype(NARROW)
    slope[...] = slope_val
    put(2, dot(w_down, act[...], 1, 0))
    send(2, 1, N)

    grad_rows = taken(1)
    grad_pre = (dot(w_down, grad_rows, 0, 0) * slope[...]).astype(NARROW)
    put(3, dot(w_up, grad_pre, 0, 0))
    send(3, 1, N)

    def chunked(value):
        return value.astype(NARROW).reshape(n_dp, value.shape[0] // n_dp, value.shape[1])

    def scatter(j):
        copies = []
        for k in range(1, n_dp):
            other = lax.rem(dp + k, n_dp)
            copy = pltpu.make_async_remote_copy(
                part.at[j, other], pieces.at[j, k - 1], scat_send.at[j, k - 1],
                scat_recv.at[j, k - 1], device_id=(other, me), device_id_type=MESH,
            )
            copy.start()
            copies.append(copy)
        return copies

    def gather(j, copies):
        value = part[j, dp].astype(WIDE)
        for k in range(1, n_dp):
            copies[k - 1].wait_recv()
            value = value + pieces[j, k - 1].astype(WIDE)
        total[j] = value.astype(NARROW)
        every[j, dp] = total[j]
        out = []
        for k in range(1, n_dp):
            other = lax.rem(dp + k, n_dp)
            copy = pltpu.make_async_remote_copy(
                total.at[j], every.at[j, dp], gath_send.at[j, k - 1],
                gath_recv.at[j, k - 1], device_id=(other, me), device_id_type=MESH,
            )
            copy.start()
            out.append(copy)
        return out

    mixed_up = dot(grad_pre, permuted, 1, 1).astype(NARROW)
    part[1] = chunked(
        jnp.concatenate([dot(mixed_up[N * b : N * b + N], pick_up[b], 1, 1) for b in range(2)], 0)
    )
    scat_up_second = scatter(1)
    mixed_down = dot(grad_rows, act[...], 1, 1).astype(NARROW)
    part[2] = chunked(
        jnp.concatenate([dot(pick_down[b], mixed_down[:, N * b : N * b + N], 1, 0) for b in range(2)], 0)
    )
    scat_down_first = scatter(2)

    def to_partner(i, value):
        halves[i] = value.reshape(2, half, tok)
        halves_out[i] = halves[i, 1 - core].astype(NARROW)
        copy = pltpu.make_async_remote_copy(
            halves_out.at[i], halves_in.at[i], half_send.at[i], half_recv.at[i],
            device_id=(dp, partner), device_id_type=MESH,
        )
        copy.start()
        return copy

    back_rows = taken(2)
    part[3] = chunked(dot(back_rows, d_block, 1, 1))
    scat_down_second = scatter(3)
    out_half = to_partner(0, dot(ds_ref[...], back_rows, 0, 0))
    gath_up_second = gather(1, scat_up_second)
    gath_down_first = gather(2, scat_down_first)

    grad_hidden = taken(3)
    part[0] = chunked(dot(grad_hidden, x_block, 1, 1))
    scat_up_first = scatter(0)
    grad_half = to_partner(1, dot(uf_ref[...], grad_hidden, 0, 0))
    gath_down_second = gather(3, scat_down_second)

    out_half.wait_recv()
    mixed_ref[...] = (
        x_ref[...].astype(WIDE) + (halves[0, core] + halves_in[0].astype(WIDE))
    ).astype(NARROW)
    grad_half.wait_recv()
    gtok_ref[...] = (
        d_ref[...].astype(WIDE) + (halves[1, core] + halves_in[1].astype(WIDE))
    ).astype(NARROW)
    gath_up_first = gather(0, scat_up_first)

    for j, copies in ((1, gath_up_second), (2, gath_down_first), (3, gath_down_second), (0, gath_up_first)):
        for copy in copies:
            copy.wait_recv()
        grads_ref[j] = every[j].reshape(rows, N)

    for copy in to_pair + [out_half, grad_half]:
        copy.wait_send()
    for copies in (
        scat_up_second, scat_down_first, scat_down_second, scat_up_first,
        gath_up_second, gath_down_first, gath_down_second, gath_up_first,
    ):
        for copy in copies:
            copy.wait_send()
    for i in range(4):
        all_of(i, send_sem).wait()


def finish(scale, mixed_in, gtok_in, grads_in, mixed_ref, gtok_ref, uf_ref, us_ref, df_ref, ds_ref):
    mixed_ref[...] = mixed_in[...]
    gtok_ref[...] = gtok_in[...]
    for j, ref in enumerate((uf_ref, us_ref, df_ref, ds_ref)):
        ref[...] = (grads_in[j].astype(WIDE) * scale).reshape(ref.shape)


def shards(tokens, cotangent, up_first, up_second, down_first, down_second, perm_up, perm_down):
    half, tok = tokens.shape
    block = up_first.shape[2]
    rows = 2 * N
    n_dp = lax.axis_size("dp")
    vmem = pl.BlockSpec(memory_space=pltpu.VMEM)
    regular = pltpu.SemaphoreType.REGULAR
    dma = pltpu.SemaphoreType.DMA
    small = jax.ShapeDtypeStruct((half, tok), NARROW)
    mixed, gtok, grads = pl.pallas_call(
        exchange,
        name="exchange",
        out_shape=(small, small, jax.ShapeDtypeStruct((4, rows, block), NARROW)),
        in_specs=[vmem] * 8,
        out_specs=(vmem,) * 3,
        scratch_shapes=[
            pltpu.VMEM((2, half, tok), NARROW),
            pltpu.VMEM((2, half, tok), NARROW),
            pltpu.VMEM((4, N, 2, tok), NARROW),
            pltpu.VMEM((4, N, 2, tok), NARROW),
            pltpu.VMEM((rows, tok), NARROW),
            pltpu.VMEM((rows, tok), WIDE),
            pltpu.VMEM((2, 2, half, tok), WIDE),
            pltpu.VMEM((2, half, tok), NARROW),
            pltpu.VMEM((2, half, tok), NARROW),
            pltpu.VMEM((4, n_dp, rows // n_dp, block), NARROW),
            pltpu.VMEM((4, n_dp - 1, rows // n_dp, block), NARROW),
            pltpu.VMEM((4, rows // n_dp, block), NARROW),
            pltpu.VMEM((4, n_dp, rows // n_dp, block), NARROW),
            regular,
            regular,
            dma((2,)),
            dma((2,)),
            dma((4,)),
            dma((4,)),
            dma((2,)),
            dma((2,)),
            dma((4, n_dp - 1)),
            dma((4, n_dp - 1)),
            dma((4, n_dp - 1)),
            dma((4, n_dp - 1)),
        ],
        compiler_params=pltpu.CompilerParams(collective_id=0, has_side_effects=True),
    )(
        tokens, cotangent, up_first.reshape(rows, block), up_second, down_first,
        down_second.reshape(rows, block), perm_up.reshape(1, N), perm_down.reshape(1, N),
    )
    scale = 1.0 / math.sqrt(n_dp * tok)
    first = jax.ShapeDtypeStruct((1, rows, block), WIDE)
    second = jax.ShapeDtypeStruct((2, block, block), WIDE)
    return pl.pallas_call(
        functools.partial(finish, scale),
        name="finish",
        out_shape=(small, small, first, second, second, first),
        in_specs=[vmem] * 3,
        out_specs=(vmem,) * 6,
    )(mixed, gtok, grads)


def solution(mesh):
    spread = P("loop", "dp")
    weight = P("loop", None, None)
    return jax.shard_map(
        shards,
        mesh=mesh,
        in_specs=(spread, spread, weight, weight, weight, weight, P(), P()),
        out_specs=(spread, spread, weight, weight, weight, weight),
        check_vma=False,
    )
```

```python
import functools
import math

import jax
import jax.numpy as jnp
from jax import lax
from jax.experimental import pallas as pl
from jax.experimental.pallas import tpu as pltpu
from jax.sharding import PartitionSpec as P

MESH = pl.DeviceIdType.MESH
WIDE = jnp.float32
NARROW = jnp.bfloat16
NX = 4
NY = 8
NZC = 4
N = NX * NY * NZC
DIRECT = (2, 3)


def dot(a, b, ca, cb):
    return lax.dot_general(a, b, (((ca,), (cb,)), ((), ())), preferred_element_type=WIDE)


def gelu_parts(pre_act):
    cumul = 0.5 * (1.0 + lax.erf(pre_act * (1.0 / math.sqrt(2.0))))
    slope = cumul + pre_act * jnp.exp(-0.5 * pre_act * pre_act) * (1.0 / math.sqrt(2.0 * math.pi))
    return (pre_act * cumul, slope)


def exchange(
    x_hbm, d_hbm, uf_hbm, us_hbm, df_hbm, ds_hbm, pu_hbm, pd_hbm,
    mixed_ref, gtok_ref, grads_ref,
    xb, db, uf_ref, us_ref, df_ref, ds_ref, pu_ref, pd_ref,
    sent, got, act, slope, halves, halves_out, halves_in,
    part, pieces, total, every, qpart, qpieces, qtotal, qevery, whole, wholes,
    near_sem, far_sem, load_sem, pair_send, pair_recv, send_sem, recv_sem, half_send, half_recv,
    scat_send, scat_recv, gath_send, gath_recv, qscat_send, qscat_recv, qgath_send, qgath_recv,
):
    me = lax.axis_index("loop")
    dp = lax.axis_index("dp")
    n_dp = lax.axis_size("dp")
    core = lax.rem(me, 2)
    zc = lax.rem(me, NZC)
    z = lax.div(zc, 2)
    y = lax.rem(lax.div(me, NZC), NY)
    x = lax.div(me, NZC * NY)
    plane = NY * NZC
    half = xb.shape[1]
    tok = xb.shape[2]
    rows = 2 * N

    def moved(dx, dy, dz, dc):
        return (
            (lax.rem(x + dx, NX) * NY + lax.rem(y + dy, NY)) * NZC
            + lax.rem(z + dz, 2) * 2
            + lax.rem(core + dc, 2)
        )

    partner = moved(0, 0, 0, 1)
    along_y = [moved(0, k, 0, 0) for k in range(1, NY)]
    along_x = [moved(k, 0, 0, 0) for k in range(1, NX)]
    along_z = [moved(0, 0, 0, 1), moved(0, 0, 1, 0), moved(0, 0, 1, 1)]

    def signal(sem, who, group):
        pl.semaphore_signal(sem, 1, device_id=(group, who), device_id_type=MESH)

    barrier = pltpu.get_barrier_semaphore()
    for who in along_y + along_x + along_z:
        signal(barrier, who, dp)
    for k in range(1, n_dp):
        signal(barrier, me, lax.rem(dp + k, n_dp))

    loads = []
    for i, (src, dst) in enumerate(
        (
            (x_hbm, xb.at[core]), (d_hbm, db.at[core]), (uf_hbm, uf_ref), (ds_hbm, ds_ref),
            (us_hbm, us_ref), (df_hbm, df_ref), (pu_hbm, pu_ref), (pd_hbm, pd_ref),
        )
    ):
        copy = pltpu.make_async_copy(src, dst, load_sem.at[i])
        copy.start()
        loads.append(copy)

    def remote(src, dst, send, recv, group, who):
        copy = pltpu.make_async_remote_copy(
            src, dst, send, recv, device_id=(group, who), device_id_type=MESH
        )
        copy.start()
        return copy

    pl.semaphore_wait(barrier, NY - 1 + NX - 1 + 3 + n_dp - 1)
    for who in along_x:
        signal(near_sem, who, dp)
    to_pair = [
        remote(src, dst.at[core], pair_send.at[i], pair_recv.at[i], dp, partner)
        for i, (src, dst) in enumerate(((x_hbm, xb), (d_hbm, db)))
    ]
    pl.semaphore_wait(near_sem, NX - 1)
    for who in along_z:
        signal(far_sem, who, dp)

    def send(i, first, last):
        def one(k, carry):
            dzc = lax.div(k, NX * NY)
            rest = lax.rem(k, NX * NY)
            who = moved(lax.div(rest, NY), lax.rem(rest, NY), lax.div(dzc, 2), lax.rem(dzc, 2))
            remote(sent.at[i, who], got.at[i, me], send_sem.at[i], recv_sem.at[i, 0], dp, who)
            return carry

        lax.fori_loop(first, last, one, 0)

    def send_planes(i):
        for dx in range(NX):

            def one(k, carry, dx=dx):
                dzc = lax.div(k, NY)
                who = moved(dx, lax.rem(k, NY), lax.div(dzc, 2), lax.rem(dzc, 2))
                remote(sent.at[i, who], got.at[i, me], send_sem.at[i], recv_sem.at[i, dx], dp, who)
                return carry

            lax.fori_loop(0 if dx else 1, plane, one, 0)

    def landed(i, count, sem):
        return pltpu.make_async_copy(sent.at[i, pl.ds(0, count)], got.at[i, pl.ds(0, count)], sem)

    def put(i, value):
        sent[i] = value.astype(NARROW).reshape(N, 2, tok)
        got[i, me] = sent[i, me]

    def taken(i):
        landed(i, N - 1, recv_sem.at[i, 0]).wait()
        return got[i].reshape(rows, tok)

    loads[0].wait()
    loads[2].wait()
    to_pair[0].wait_recv()
    x_block = xb[...].reshape(2 * half, tok)
    put(0, dot(uf_ref[...], x_block, 1, 0))
    send(0, 1, NX * NY)
    loads[1].wait()
    loads[3].wait()
    to_pair[1].wait_recv()
    d_block = db[...].reshape(2 * half, tok)
    put(1, dot(ds_ref[...], d_block, 1, 0))
    pl.semaphore_wait(far_sem, 3)
    send(0, NX * NY, N)
    send(1, 1, N)

    for copy in loads[4:]:
        copy.wait()
    down = lax.broadcasted_iota(jnp.int32, (N, N), 0)
    row_up = (down == pu_ref[...]).astype(NARROW)
    row_down = (down == pd_ref[...]).astype(NARROW)
    lane = lax.broadcasted_iota(jnp.int32, (N, rows), 1)
    sub = lax.broadcasted_iota(jnp.int32, (N, rows), 0)
    spread = [(lane == 2 * sub + b).astype(NARROW) for b in range(2)]
    pick_up = [dot(row_up, e, 0, 0).astype(NARROW) for e in spread]
    pick_down = [dot(row_down, e, 1, 0).astype(NARROW) for e in spread]
    w_up = jnp.concatenate([dot(us_ref[b], pick_up[b], 1, 0).astype(NARROW) for b in range(2)], 0)
    w_down = jnp.concatenate(
        [dot(pick_down[b], df_ref[b], 0, 0).astype(NARROW) for b in range(2)], 1
    )

    permuted = taken(0)
    gelu_val, slope_val = gelu_parts(dot(w_up, permuted, 1, 0))
    act[...] = gelu_val.astype(NARROW)
    slope[...] = slope_val
    put(2, dot(w_down, act[...], 1, 0))
    send_planes(2)

    grad_rows = taken(1)
    grad_pre = (dot(w_down, grad_rows, 0, 0) * slope[...]).astype(NARROW)
    put(3, dot(w_up, grad_pre, 0, 0))
    send_planes(3)

    others = [lax.rem(dp + k, n_dp) for k in range(1, n_dp)]
    sends = list(to_pair)

    def spread_out(own, slots, send_at, recv_at):
        copies = [
            remote(own(other), slots(k), send_at.at[k], recv_at.at[k], other, me)
            for k, other in enumerate(others)
        ]
        sends.extend(copies)
        return copies

    def scatter(src, dst, send_at, recv_at):
        return spread_out(lambda other: src.at[other], lambda k: dst.at[k], send_at, recv_at)

    def gather(copies, src, landing, sums, dst, send_at, recv_at):
        value = src[dp].astype(WIDE)
        for k, copy in enumerate(copies):
            copy.wait_recv()
            value = value + landing[k].astype(WIDE)
        sums[...] = value.astype(NARROW)
        dst[dp] = sums[...]
        return spread_out(lambda other: sums, lambda k: dst.at[dp], send_at, recv_at)

    def chunked(value):
        return value.astype(NARROW).reshape(n_dp, value.shape[0] // n_dp, value.shape[1])

    def scatter_block(j):
        return scatter(part.at[j], pieces.at[j], scat_send.at[j], scat_recv.at[j])

    def gather_block(j, copies):
        return gather(
            copies, part.at[j], pieces.at[j], total.at[j], every.at[j], gath_send.at[j], gath_recv.at[j]
        )

    def scatter_plane(s, q):
        return scatter(qpart.at[s, q], qpieces.at[s, q], qscat_send.at[s, q], qscat_recv.at[s, q])

    def gather_plane(s, q, copies):
        return gather(
            copies, qpart.at[s, q], qpieces.at[s, q], qtotal.at[s, q], qevery.at[s, q],
            qgath_send.at[s, q], qgath_recv.at[s, q],
        )

    def plane_of(q):
        return lax.rem(x + NX - q, NX)

    def plane_rows(i, q):
        landed(i, plane if q else plane - 1, recv_sem.at[i, q]).wait()
        return got[i, pl.ds(plane_of(q) * plane, plane)].reshape(2 * plane, tok)

    mixed_up = dot(grad_pre, permuted, 1, 1).astype(NARROW)
    part[0] = chunked(
        jnp.concatenate([dot(mixed_up[N * b : N * b + N], pick_up[b], 1, 1) for b in range(2)], 0)
    )
    scat_up = scatter_block(0)
    mixed_down = dot(grad_rows, act[...], 1, 1).astype(NARROW)
    part[1] = chunked(
        jnp.concatenate([dot(pick_down[b], mixed_down[:, N * b : N * b + N], 1, 0) for b in range(2)], 0)
    )
    scat_down = scatter_block(1)

    def to_partner(i, value):
        halves[i] = value.reshape(2, half, tok)
        halves_out[i] = halves[i, 1 - core].astype(NARROW)
        copy = remote(halves_out.at[i], halves_in.at[i], half_send.at[i], half_recv.at[i], dp, partner)
        sends.append(copy)
        return copy

    def joined(i, base, copy):
        copy.wait_recv()
        return (
            base[core].astype(WIDE) + (halves[i, core] + halves_in[i].astype(WIDE))
        ).astype(NARROW)

    def plane_grad(s, q, block):
        value = dot(plane_rows(2 + s, q), block, 1, 1)
        if s == 1 and q in DIRECT:
            whole[q] = value.astype(NARROW)
            wholes[q, dp] = whole[q]
            return spread_out(
                lambda other: whole.at[q], lambda k: wholes.at[q, dp], qscat_send.at[s, q],
                qscat_recv.at[s, q],
            )
        qpart[s, q] = chunked(value)
        return scatter_plane(s, q)

    scat_second = [plane_grad(0, q, d_block) for q in range(NX)]
    out_half = to_partner(0, dot(ds_ref[...], got[2].reshape(rows, tok), 0, 0))
    gath_up = gather_block(0, scat_up)
    gath_down = gather_block(1, scat_down)
    scat_first = [plane_grad(1, 0, x_block), plane_grad(1, 1, x_block)]
    gath_second = [gather_plane(0, q, scat_second[q]) for q in range(NX)]
    scat_first += [plane_grad(1, q, x_block) for q in range(2, NX)]
    grad_half = to_partner(1, dot(uf_ref[...], got[3].reshape(rows, tok), 0, 0))
    mixed_ref[...] = joined(0, xb, out_half)
    gath_first = [None if q in DIRECT else gather_plane(1, q, scat_first[q]) for q in range(NX)]
    gtok_ref[...] = joined(1, db, grad_half)

    for j, copies in ((0, gath_up), (1, gath_down)):
        for copy in copies:
            copy.wait_recv()
        grads_ref[1 + j] = every[j].reshape(NX, 2 * plane, N)
    for s, j, found in ((0, 3, gath_second), (1, 0, gath_first)):
        for q in range(NX):
            for copy in found[q] or scat_first[q]:
                copy.wait_recv()
            if found[q]:
                grads_ref[j, plane_of(q)] = qevery[s, q].reshape(2 * plane, N)
            else:
                value = wholes[q, 0].astype(WIDE)
                for k in range(1, n_dp):
                    value = value + wholes[q, k].astype(WIDE)
                grads_ref[j, plane_of(q)] = value.astype(NARROW)

    for copy in sends:
        copy.wait_send()
    for i in range(4):
        landed(i, N - 1, send_sem.at[i]).wait()


def finish(scale, mixed_in, gtok_in, grads_in, mixed_ref, gtok_ref, uf_ref, us_ref, df_ref, ds_ref):
    mixed_ref[...] = mixed_in[...]
    gtok_ref[...] = gtok_in[...]
    for j, ref in enumerate((uf_ref, us_ref, df_ref, ds_ref)):
        ref[...] = (grads_in[j].astype(WIDE) * scale).reshape(ref.shape)


def shards(tokens, cotangent, up_first, up_second, down_first, down_second, perm_up, perm_down):
    half, tok = tokens.shape
    block = up_first.shape[2]
    rows = 2 * N
    n_dp = lax.axis_size("dp")
    vmem = pl.BlockSpec(memory_space=pltpu.VMEM)
    regular = pltpu.SemaphoreType.REGULAR
    dma = pltpu.SemaphoreType.DMA
    small = jax.ShapeDtypeStruct((half, tok), NARROW)
    some = rows // n_dp
    few = some // NX
    mixed, gtok, grads = pl.pallas_call(
        exchange,
        name="exchange",
        out_shape=(
            pltpu.VMEM((half, tok), NARROW),
            pltpu.VMEM((half, tok), NARROW),
            pltpu.VMEM((4, NX, rows // NX, block), NARROW),
        ),
        in_specs=[pl.BlockSpec(memory_space=pl.ANY)] * 8,
        out_specs=(vmem,) * 3,
        scratch_shapes=[
            pltpu.VMEM((2, half, tok), NARROW),
            pltpu.VMEM((2, half, tok), NARROW),
            pltpu.VMEM((rows, block), NARROW),
            pltpu.VMEM((2, block, block), NARROW),
            pltpu.VMEM((2, block, block), NARROW),
            pltpu.VMEM((rows, block), NARROW),
            pltpu.VMEM((1, N), jnp.int32),
            pltpu.VMEM((1, N), jnp.int32),
            pltpu.VMEM((4, N, 2, tok), NARROW),
            pltpu.VMEM((4, N, 2, tok), NARROW),
            pltpu.VMEM((rows, tok), NARROW),
            pltpu.VMEM((rows, tok), WIDE),
            pltpu.VMEM((2, 2, half, tok), WIDE),
            pltpu.VMEM((2, half, tok), NARROW),
            pltpu.VMEM((2, half, tok), NARROW),
            pltpu.VMEM((2, n_dp, some, block), NARROW),
            pltpu.VMEM((2, n_dp - 1, some, block), NARROW),
            pltpu.VMEM((2, some, block), NARROW),
            pltpu.VMEM((2, n_dp, some, block), NARROW),
            pltpu.VMEM((2, NX, n_dp, few, block), NARROW),
            pltpu.VMEM((2, NX, n_dp - 1, few, block), NARROW),
            pltpu.VMEM((2, NX, few, block), NARROW),
            pltpu.VMEM((2, NX, n_dp, few, block), NARROW),
            pltpu.VMEM((NX, rows // NX, block), NARROW),
            pltpu.VMEM((NX, n_dp, rows // NX, block), NARROW),
            regular,
            regular,
            dma((8,)),
            dma((2,)),
            dma((2,)),
            dma((4,)),
            dma((4, NX)),
            dma((2,)),
            dma((2,)),
            *(dma((2, n_dp - 1)),) * 4,
            *(dma((2, NX, n_dp - 1)),) * 4,
        ],
        compiler_params=pltpu.CompilerParams(collective_id=0, has_side_effects=True),
    )(
        tokens, cotangent, up_first.reshape(rows, block), up_second, down_first,
        down_second.reshape(rows, block), perm_up.reshape(1, N), perm_down.reshape(1, N),
    )
    scale = 1.0 / math.sqrt(n_dp * tok)
    first = jax.ShapeDtypeStruct((1, rows, block), WIDE)
    second = jax.ShapeDtypeStruct((2, block, block), WIDE)
    return pl.pallas_call(
        functools.partial(finish, scale),
        name="finish",
        out_shape=(small, small, first, second, second, first),
        in_specs=[vmem] * 3,
        out_specs=(vmem,) * 6,
    )(*(pltpu.with_memory_space_constraint(v, pltpu.VMEM) for v in (mixed, gtok, grads)))


def solution(mesh):
    spread = P("loop", "dp")
    weight = P("loop", None, None)
    return jax.shard_map(
        shards,
        mesh=mesh,
        in_specs=(spread, spread, weight, weight, weight, weight, P(), P()),
        out_specs=(spread, spread, weight, weight, weight, weight),
        check_vma=False,
    )
```

```python
import functools
import math

import jax
import jax.numpy as jnp
from jax import lax
from jax.experimental import pallas as pl
from jax.experimental.pallas import tpu as pltpu
from jax.sharding import PartitionSpec as P

MESH = pl.DeviceIdType.MESH
WIDE = jnp.float32
NARROW = jnp.bfloat16
NX = 4
NY = 8
NZC = 4
N = NX * NY * NZC
DIRECT = (2, 3)


def dot(a, b, ca, cb):
    return lax.dot_general(a, b, (((ca,), (cb,)), ((), ())), preferred_element_type=WIDE)


def gelu_parts(pre_act):
    cumul = 0.5 * (1.0 + lax.erf(pre_act * (1.0 / math.sqrt(2.0))))
    slope = cumul + pre_act * jnp.exp(-0.5 * pre_act * pre_act) * (1.0 / math.sqrt(2.0 * math.pi))
    return (pre_act * cumul, slope)


def exchange(
    x_hbm, d_hbm, uf_hbm, us_hbm, df_hbm, ds_hbm, pu_hbm, pd_hbm,
    mixed_ref, gtok_ref, grads_ref,
    xb, db, uf_ref, us_ref, df_ref, ds_ref, pu_ref, pd_ref,
    sent, got, act, slope, halves, halves_out, halves_in,
    part, pieces, total, every, qpart, qpieces, qtotal, qevery, whole, wholes,
    near_sem, far_sem, shard_sem, load_sem, pair_send, pair_recv, send_sem, recv_sem, half_send, half_recv,
    scat_send, scat_recv, gath_send, gath_recv, qscat_send, qscat_recv, qgath_send, qgath_recv,
):
    me = lax.axis_index("loop")
    dp = lax.axis_index("dp")
    n_dp = lax.axis_size("dp")
    core = lax.rem(me, 2)
    zc = lax.rem(me, NZC)
    z = lax.div(zc, 2)
    y = lax.rem(lax.div(me, NZC), NY)
    x = lax.div(me, NZC * NY)
    plane = NY * NZC
    half = xb.shape[1]
    tok = xb.shape[2]
    rows = 2 * N

    def moved(dx, dy, dz, dc):
        return (
            (lax.rem(x + dx, NX) * NY + lax.rem(y + dy, NY)) * NZC
            + lax.rem(z + dz, 2) * 2
            + lax.rem(core + dc, 2)
        )

    partner = moved(0, 0, 0, 1)
    along_y = [moved(0, k, 0, 0) for k in range(1, NY)]
    along_x = [moved(k, 0, 0, 0) for k in range(1, NX)]
    along_z = [moved(0, 0, 0, 1), moved(0, 0, 1, 0), moved(0, 0, 1, 1)]

    def signal(sem, who, group):
        pl.semaphore_signal(sem, 1, device_id=(group, who), device_id_type=MESH)

    barrier = pltpu.get_barrier_semaphore()
    for who in along_y + along_x + along_z:
        signal(barrier, who, dp)
    for k in range(1, n_dp):

        @pl.when(dp + k < n_dp)
        def _(k=k):
            signal(barrier, me, dp + k)

    loads = []
    for i, (src, dst) in enumerate(
        (
            (x_hbm, xb.at[core]), (d_hbm, db.at[core]), (uf_hbm, uf_ref), (ds_hbm, ds_ref),
            (us_hbm, us_ref), (df_hbm, df_ref), (pu_hbm, pu_ref), (pd_hbm, pd_ref),
        )
    ):
        copy = pltpu.make_async_copy(src, dst, load_sem.at[i])
        copy.start()
        loads.append(copy)

    def remote(src, dst, send, recv, group, who):
        copy = pltpu.make_async_remote_copy(
            src, dst, send, recv, device_id=(group, who), device_id_type=MESH
        )
        copy.start()
        return copy

    pl.semaphore_wait(barrier, NY - 1 + NX - 1 + 3 + dp)
    for who in along_z:
        signal(near_sem, who, dp)
    to_pair = [
        remote(src, dst.at[core], pair_send.at[i], pair_recv.at[i], dp, partner)
        for i, (src, dst) in enumerate(((x_hbm, xb), (d_hbm, db)))
    ]
    pl.semaphore_wait(near_sem, 3)
    for who in along_x:
        signal(far_sem, who, dp)
    for k in range(1, n_dp):

        @pl.when(dp >= k)
        def _(k=k):
            signal(shard_sem, me, dp - k)

    spot = lax.rem(me, plane)

    def send(i, planes, apart=True):
        for dx in planes:
            base = lax.rem(x + dx, NX) * plane

            def one(k, carry, dx=dx, base=base):
                who = base + lax.rem(spot + k, plane)
                arrived = recv_sem.at[i, dx if apart else 0]
                remote(sent.at[i, who], got.at[i, me], send_sem.at[i], arrived, dp, who)
                return carry

            lax.fori_loop(0 if dx else 1, plane, one, 0)

    def landed(i, count, sem):
        return pltpu.make_async_copy(sent.at[i, pl.ds(0, count)], got.at[i, pl.ds(0, count)], sem)

    def put(i, value):
        sent[i] = value.astype(NARROW).reshape(N, 2, tok)
        got[i, me] = sent[i, me]

    def taken(i):
        landed(i, N - 1, recv_sem.at[i, 0]).wait()
        return got[i].reshape(rows, tok)

    loads[0].wait()
    loads[2].wait()
    to_pair[0].wait_recv()
    x_block = xb[...].reshape(2 * half, tok)
    put(0, dot(uf_ref[...], x_block, 1, 0))
    send(0, (0,), False)
    loads[1].wait()
    loads[3].wait()
    to_pair[1].wait_recv()
    d_block = db[...].reshape(2 * half, tok)
    put(1, dot(ds_ref[...], d_block, 1, 0))
    pl.semaphore_wait(far_sem, NX - 1)
    send(0, range(1, NX), False)
    send(1, range(NX), False)

    for copy in loads[4:]:
        copy.wait()
    down = lax.broadcasted_iota(jnp.int32, (N, N), 0)
    row_up = (down == pu_ref[...]).astype(NARROW)
    row_down = (down == pd_ref[...]).astype(NARROW)
    lane = lax.broadcasted_iota(jnp.int32, (N, rows), 1)
    sub = lax.broadcasted_iota(jnp.int32, (N, rows), 0)
    spread = [(lane == 2 * sub + b).astype(NARROW) for b in range(2)]
    pick_up = [dot(row_up, e, 0, 0).astype(NARROW) for e in spread]
    pick_down = [dot(row_down, e, 1, 0).astype(NARROW) for e in spread]
    w_up = jnp.concatenate([dot(us_ref[b], pick_up[b], 1, 0).astype(NARROW) for b in range(2)], 0)
    w_down = jnp.concatenate(
        [dot(pick_down[b], df_ref[b], 0, 0).astype(NARROW) for b in range(2)], 1
    )

    permuted = taken(0)
    gelu_val, slope_val = gelu_parts(dot(w_up, permuted, 1, 0))
    act[...] = gelu_val.astype(NARROW)
    slope[...] = slope_val
    put(2, dot(w_down, act[...], 1, 0))
    send(2, range(NX))

    grad_rows = taken(1)
    grad_pre = (dot(w_down, grad_rows, 0, 0) * slope[...]).astype(NARROW)
    put(3, dot(w_up, grad_pre, 0, 0))
    send(3, range(NX))

    @pl.when(dp + 1 < n_dp)
    def _():
        pl.semaphore_wait(shard_sem, n_dp - 1 - dp)


    others = [lax.rem(dp + k, n_dp) for k in range(1, n_dp)]
    sends = list(to_pair)

    def spread_out(own, slots, send_at, recv_at):
        copies = [
            remote(own(other), slots(k), send_at.at[k], recv_at.at[k], other, me)
            for k, other in enumerate(others)
        ]
        sends.extend(copies)
        return copies

    def scatter(src, dst, send_at, recv_at):
        return spread_out(lambda other: src.at[other], lambda k: dst.at[k], send_at, recv_at)

    def gather(copies, src, landing, sums, dst, send_at, recv_at):
        value = src[dp].astype(WIDE)
        for k, copy in enumerate(copies):
            copy.wait_recv()
            value = value + landing[k].astype(WIDE)
        sums[...] = value.astype(NARROW)
        dst[dp] = sums[...]
        return spread_out(lambda other: sums, lambda k: dst.at[dp], send_at, recv_at)

    def chunked(value):
        return value.astype(NARROW).reshape(n_dp, value.shape[0] // n_dp, value.shape[1])

    def scatter_block(j):
        return scatter(part.at[j], pieces.at[j], scat_send.at[j], scat_recv.at[j])

    def gather_block(j, copies):
        return gather(
            copies, part.at[j], pieces.at[j], total.at[j], every.at[j], gath_send.at[j], gath_recv.at[j]
        )

    def scatter_plane(s, q):
        return scatter(qpart.at[s, q], qpieces.at[s, q], qscat_send.at[s, q], qscat_recv.at[s, q])

    def gather_plane(s, q, copies):
        return gather(
            copies, qpart.at[s, q], qpieces.at[s, q], qtotal.at[s, q], qevery.at[s, q],
            qgath_send.at[s, q], qgath_recv.at[s, q],
        )

    def plane_of(q):
        return lax.rem(x + NX - q, NX)

    def plane_rows(i, q):
        landed(i, plane if q else plane - 1, recv_sem.at[i, q]).wait()
        return got[i, pl.ds(plane_of(q) * plane, plane)].reshape(2 * plane, tok)

    mixed_up = dot(grad_pre, permuted, 1, 1).astype(NARROW)
    part[0] = chunked(
        jnp.concatenate([dot(mixed_up[N * b : N * b + N], pick_up[b], 1, 1) for b in range(2)], 0)
    )
    scat_up = scatter_block(0)
    mixed_down = dot(grad_rows, act[...], 1, 1).astype(NARROW)
    part[1] = chunked(
        jnp.concatenate([dot(pick_down[b], mixed_down[:, N * b : N * b + N], 1, 0) for b in range(2)], 0)
    )
    scat_down = scatter_block(1)

    def to_partner(i, value):
        halves[i] = value.reshape(2, half, tok)
        halves_out[i] = halves[i, 1 - core].astype(NARROW)
        copy = remote(halves_out.at[i], halves_in.at[i], half_send.at[i], half_recv.at[i], dp, partner)
        sends.append(copy)
        return copy

    def joined(i, base, copy):
        copy.wait_recv()
        return (
            base[core].astype(WIDE) + (halves[i, core] + halves_in[i].astype(WIDE))
        ).astype(NARROW)

    def plane_grad(s, q, block):
        value = dot(plane_rows(2 + s, q), block, 1, 1)
        if s == 1 and q in DIRECT:
            whole[q] = value.astype(NARROW)
            wholes[q, dp] = whole[q]
            return spread_out(
                lambda other: whole.at[q], lambda k: wholes.at[q, dp], qscat_send.at[s, q],
                qscat_recv.at[s, q],
            )
        qpart[s, q] = chunked(value)
        return scatter_plane(s, q)

    scat_second = [plane_grad(0, q, d_block) for q in range(NX)]
    out_half = to_partner(0, dot(ds_ref[...], got[2].reshape(rows, tok), 0, 0))
    gath_up = gather_block(0, scat_up)
    gath_down = gather_block(1, scat_down)
    scat_first = [plane_grad(1, 0, x_block), plane_grad(1, 1, x_block)]
    gath_second = [gather_plane(0, q, scat_second[q]) for q in range(NX)]
    scat_first += [plane_grad(1, q, x_block) for q in range(2, NX)]
    grad_half = to_partner(1, dot(uf_ref[...], got[3].reshape(rows, tok), 0, 0))
    mixed_ref[...] = joined(0, xb, out_half)
    gath_first = [None if q in DIRECT else gather_plane(1, q, scat_first[q]) for q in range(NX)]
    gtok_ref[...] = joined(1, db, grad_half)

    for j, copies in ((0, gath_up), (1, gath_down)):
        for copy in copies:
            copy.wait_recv()
        grads_ref[1 + j] = every[j].reshape(NX, 2 * plane, N)
    for s, j, found in ((0, 3, gath_second), (1, 0, gath_first)):
        for q in range(NX):
            for copy in found[q] or scat_first[q]:
                copy.wait_recv()
            if found[q]:
                grads_ref[j, plane_of(q)] = qevery[s, q].reshape(2 * plane, N)
            else:
                value = wholes[q, 0].astype(WIDE)
                for k in range(1, n_dp):
                    value = value + wholes[q, k].astype(WIDE)
                grads_ref[j, plane_of(q)] = value.astype(NARROW)

    for copy in sends:
        copy.wait_send()
    for i in range(4):
        landed(i, N - 1, send_sem.at[i]).wait()


def finish(scale, mixed_in, gtok_in, grads_in, mixed_ref, gtok_ref, uf_ref, us_ref, df_ref, ds_ref):
    mixed_ref[...] = mixed_in[...]
    gtok_ref[...] = gtok_in[...]
    for j, ref in enumerate((uf_ref, us_ref, df_ref, ds_ref)):
        ref[...] = (grads_in[j].astype(WIDE) * scale).reshape(ref.shape)


def shards(tokens, cotangent, up_first, up_second, down_first, down_second, perm_up, perm_down):
    half, tok = tokens.shape
    block = up_first.shape[2]
    rows = 2 * N
    n_dp = lax.axis_size("dp")
    vmem = pl.BlockSpec(memory_space=pltpu.VMEM)
    regular = pltpu.SemaphoreType.REGULAR
    dma = pltpu.SemaphoreType.DMA
    small = jax.ShapeDtypeStruct((half, tok), NARROW)
    some = rows // n_dp
    few = some // NX
    mixed, gtok, grads = pl.pallas_call(
        exchange,
        name="exchange",
        out_shape=(
            pltpu.VMEM((half, tok), NARROW),
            pltpu.VMEM((half, tok), NARROW),
            pltpu.VMEM((4, NX, rows // NX, block), NARROW),
        ),
        in_specs=[pl.BlockSpec(memory_space=pl.ANY)] * 8,
        out_specs=(vmem,) * 3,
        scratch_shapes=[
            pltpu.VMEM((2, half, tok), NARROW),
            pltpu.VMEM((2, half, tok), NARROW),
            pltpu.VMEM((rows, block), NARROW),
            pltpu.VMEM((2, block, block), NARROW),
            pltpu.VMEM((2, block, block), NARROW),
            pltpu.VMEM((rows, block), NARROW),
            pltpu.VMEM((1, N), jnp.int32),
            pltpu.VMEM((1, N), jnp.int32),
            pltpu.VMEM((4, N, 2, tok), NARROW),
            pltpu.VMEM((4, N, 2, tok), NARROW),
            pltpu.VMEM((rows, tok), NARROW),
            pltpu.VMEM((rows, tok), WIDE),
            pltpu.VMEM((2, 2, half, tok), WIDE),
            pltpu.VMEM((2, half, tok), NARROW),
            pltpu.VMEM((2, half, tok), NARROW),
            pltpu.VMEM((2, n_dp, some, block), NARROW),
            pltpu.VMEM((2, n_dp - 1, some, block), NARROW),
            pltpu.VMEM((2, some, block), NARROW),
            pltpu.VMEM((2, n_dp, some, block), NARROW),
            pltpu.VMEM((2, NX, n_dp, few, block), NARROW),
            pltpu.VMEM((2, NX, n_dp - 1, few, block), NARROW),
            pltpu.VMEM((2, NX, few, block), NARROW),
            pltpu.VMEM((2, NX, n_dp, few, block), NARROW),
            pltpu.VMEM((NX, rows // NX, block), NARROW),
            pltpu.VMEM((NX, n_dp, rows // NX, block), NARROW),
            regular,
            regular,
            regular,
            dma((8,)),
            dma((2,)),
            dma((2,)),
            dma((4,)),
            dma((4, NX)),
            dma((2,)),
            dma((2,)),
            *(dma((2, n_dp - 1)),) * 4,
            *(dma((2, NX, n_dp - 1)),) * 4,
        ],
        compiler_params=pltpu.CompilerParams(collective_id=0, has_side_effects=True),
    )(
        tokens, cotangent, up_first.reshape(rows, block), up_second, down_first,
        down_second.reshape(rows, block), perm_up.reshape(1, N), perm_down.reshape(1, N),
    )
    scale = 1.0 / math.sqrt(n_dp * tok)
    first = jax.ShapeDtypeStruct((1, rows, block), WIDE)
    second = jax.ShapeDtypeStruct((2, block, block), WIDE)
    return pl.pallas_call(
        functools.partial(finish, scale),
        name="finish",
        out_shape=(small, small, first, second, second, first),
        in_specs=[vmem] * 3,
        out_specs=(vmem,) * 6,
    )(*(pltpu.with_memory_space_constraint(v, pltpu.VMEM) for v in (mixed, gtok, grads)))


def solution(mesh):
    spread = P("loop", "dp")
    weight = P("loop", None, None)
    return jax.shard_map(
        shards,
        mesh=mesh,
        in_specs=(spread, spread, weight, weight, weight, weight, P(), P()),
        out_specs=(spread, spread, weight, weight, weight, weight),
        check_vma=False,
    )
```

```python
import functools
import math

import jax
import jax.numpy as jnp
from jax import lax
from jax.experimental import pallas as pl
from jax.experimental.pallas import tpu as pltpu
from jax.sharding import PartitionSpec as P

MESH = pl.DeviceIdType.MESH
WIDE = jnp.float32
NARROW = jnp.bfloat16
NX = 4
NY = 8
NZC = 4
N = NX * NY * NZC
DIRECT = (2, 3)


def dot(a, b, ca, cb):
    return lax.dot_general(a, b, (((ca,), (cb,)), ((), ())), preferred_element_type=WIDE)


def gelu_parts(pre_act):
    cumul = 0.5 * (1.0 + lax.erf(pre_act * (1.0 / math.sqrt(2.0))))
    slope = cumul + pre_act * jnp.exp(-0.5 * pre_act * pre_act) * (1.0 / math.sqrt(2.0 * math.pi))
    return (pre_act * cumul, slope)


def exchange(
    x_hbm, d_hbm, uf_hbm, us_hbm, df_hbm, ds_hbm, pu_hbm, pd_hbm,
    mixed_ref, gtok_ref, grads_ref,
    xb, db, uf_ref, us_ref, df_ref, ds_ref, pu_ref, pd_ref,
    sent, got, act, slope, halves, halves_out, halves_in,
    part, pieces, total, every, qpart, qpieces, qtotal, qevery, whole, wholes,
    near_sem, far_sem, shard_sem, load_sem, pair_send, pair_recv, send_sem, recv_sem, half_send, half_recv,
    scat_send, scat_recv, gath_send, gath_recv, qscat_send, qscat_recv, qgath_send, qgath_recv,
):
    me = lax.axis_index("loop")
    dp = lax.axis_index("dp")
    n_dp = lax.axis_size("dp")
    core = lax.rem(me, 2)
    zc = lax.rem(me, NZC)
    z = lax.div(zc, 2)
    y = lax.rem(lax.div(me, NZC), NY)
    x = lax.div(me, NZC * NY)
    plane = NY * NZC
    half = xb.shape[1]
    tok = xb.shape[2]
    rows = 2 * N

    def moved(dx, dy, dz, dc):
        return (
            (lax.rem(x + dx, NX) * NY + lax.rem(y + dy, NY)) * NZC
            + lax.rem(z + dz, 2) * 2
            + lax.rem(core + dc, 2)
        )

    partner = moved(0, 0, 0, 1)
    along_y = [moved(0, k, 0, 0) for k in range(1, NY)]
    along_x = [moved(k, 0, 0, 0) for k in range(1, NX)]
    along_z = [moved(0, 0, 0, 1), moved(0, 0, 1, 0), moved(0, 0, 1, 1)]

    def signal(sem, who, group):
        pl.semaphore_signal(sem, 1, device_id=(group, who), device_id_type=MESH)

    barrier = pltpu.get_barrier_semaphore()
    for who in along_y + along_x + along_z:
        signal(barrier, who, dp)
    for k in range(1, n_dp):

        @pl.when(dp + k < n_dp)
        def _(k=k):
            signal(barrier, me, dp + k)

    loads = []
    for i, (src, dst) in enumerate(
        (
            (x_hbm, xb.at[core]), (d_hbm, db.at[core]), (uf_hbm, uf_ref), (ds_hbm, ds_ref),
            (us_hbm, us_ref), (df_hbm, df_ref), (pu_hbm, pu_ref), (pd_hbm, pd_ref),
        )
    ):
        copy = pltpu.make_async_copy(src, dst, load_sem.at[i])
        copy.start()
        loads.append(copy)

    def remote(src, dst, send, recv, group, who):
        copy = pltpu.make_async_remote_copy(
            src, dst, send, recv, device_id=(group, who), device_id_type=MESH
        )
        copy.start()
        return copy

    pl.semaphore_wait(barrier, NY - 1 + NX - 1 + 3 + dp)
    for who in along_z:
        signal(near_sem, who, dp)
    to_pair = [
        remote(src, dst.at[core], pair_send.at[i], pair_recv.at[i], dp, partner)
        for i, (src, dst) in enumerate(((x_hbm, xb), (d_hbm, db)))
    ]
    pl.semaphore_wait(near_sem, 3)
    for who in along_x:
        signal(far_sem, who, dp)
    for k in range(1, n_dp):

        @pl.when(dp >= k)
        def _(k=k):
            signal(shard_sem, me, dp - k)

    spot = lax.rem(me, plane)

    def send(i, planes, apart=True):
        for dx in planes:
            base = lax.rem(x + dx, NX) * plane

            def one(k, carry, dx=dx, base=base):
                who = base + lax.rem(spot + k, plane)
                arrived = recv_sem.at[i, dx if apart else 0]
                remote(sent.at[i, who], got.at[i, me], send_sem.at[i], arrived, dp, who)
                return carry

            lax.fori_loop(0 if dx else 1, plane, one, 0)

    def landed(i, count, sem):
        return pltpu.make_async_copy(sent.at[i, pl.ds(0, count)], got.at[i, pl.ds(0, count)], sem)

    def put(i, value):
        sent[i] = value.astype(NARROW).reshape(N, 2, tok)
        got[i, me] = sent[i, me]

    def taken(i):
        landed(i, N - 1, recv_sem.at[i, 0]).wait()
        return got[i].reshape(rows, tok)

    loads[0].wait()
    loads[2].wait()
    to_pair[0].wait_recv()
    x_block = xb[...].reshape(2 * half, tok)
    put(0, dot(uf_ref[...], x_block, 1, 0))
    send(0, (0,), False)
    loads[1].wait()
    loads[3].wait()
    to_pair[1].wait_recv()
    d_block = db[...].reshape(2 * half, tok)
    put(1, dot(ds_ref[...], d_block, 1, 0))
    pl.semaphore_wait(far_sem, NX - 1)
    send(0, range(1, NX), False)
    send(1, range(NX), False)

    for copy in loads[4:]:
        copy.wait()
    down = lax.broadcasted_iota(jnp.int32, (N, N), 0)
    row_up = (down == pu_ref[...]).astype(NARROW)
    row_down = (down == pd_ref[...]).astype(NARROW)
    lane = lax.broadcasted_iota(jnp.int32, (N, rows), 1)
    sub = lax.broadcasted_iota(jnp.int32, (N, rows), 0)
    spread = [(lane == 2 * sub + b).astype(NARROW) for b in range(2)]
    pick_up = [dot(row_up, e, 0, 0).astype(NARROW) for e in spread]
    pick_down = [dot(row_down, e, 1, 0).astype(NARROW) for e in spread]
    w_up = jnp.concatenate([dot(us_ref[b], pick_up[b], 1, 0).astype(NARROW) for b in range(2)], 0)
    w_down = jnp.concatenate(
        [dot(pick_down[b], df_ref[b], 0, 0).astype(NARROW) for b in range(2)], 1
    )

    permuted = taken(0)
    gelu_val, slope_val = gelu_parts(dot(w_up, permuted, 1, 0))
    act[...] = gelu_val.astype(NARROW)
    slope[...] = slope_val
    put(2, dot(w_down, act[...], 1, 0))
    send(2, range(NX))

    others = [lax.rem(dp + k, n_dp) for k in range(1, n_dp)]
    sends = list(to_pair)

    def spread_out(own, slots, send_at, recv_at):
        copies = [
            remote(own(other), slots(k), send_at.at[k], recv_at.at[k], other, me)
            for k, other in enumerate(others)
        ]
        sends.extend(copies)
        return copies

    def scatter(src, dst, send_at, recv_at):
        return spread_out(lambda other: src.at[other], lambda k: dst.at[k], send_at, recv_at)

    def gather(copies, src, landing, sums, dst, send_at, recv_at):
        value = src[dp].astype(WIDE)
        for k, copy in enumerate(copies):
            copy.wait_recv()
            value = value + landing[k].astype(WIDE)
        sums[...] = value.astype(NARROW)
        dst[dp] = sums[...]
        return spread_out(lambda other: sums, lambda k: dst.at[dp], send_at, recv_at)

    def chunked(value):
        return value.astype(NARROW).reshape(n_dp, value.shape[0] // n_dp, value.shape[1])

    def scatter_block(j):
        return scatter(part.at[j], pieces.at[j], scat_send.at[j], scat_recv.at[j])

    def gather_block(j, copies):
        return gather(
            copies, part.at[j], pieces.at[j], total.at[j], every.at[j], gath_send.at[j], gath_recv.at[j]
        )

    def scatter_plane(s, q):
        return scatter(qpart.at[s, q], qpieces.at[s, q], qscat_send.at[s, q], qscat_recv.at[s, q])

    def gather_plane(s, q, copies):
        return gather(
            copies, qpart.at[s, q], qpieces.at[s, q], qtotal.at[s, q], qevery.at[s, q],
            qgath_send.at[s, q], qgath_recv.at[s, q],
        )

    def plane_of(q):
        return lax.rem(x + NX - q, NX)

    def plane_rows(i, q):
        landed(i, plane if q else plane - 1, recv_sem.at[i, q]).wait()
        return got[i, pl.ds(plane_of(q) * plane, plane)].reshape(2 * plane, tok)

    grad_rows = taken(1)
    @pl.when(dp + 1 < n_dp)
    def _():
        pl.semaphore_wait(shard_sem, n_dp - 1 - dp)


    mixed_down = dot(grad_rows, act[...], 1, 1).astype(NARROW)
    part[1] = chunked(
        jnp.concatenate([dot(pick_down[b], mixed_down[:, N * b : N * b + N], 1, 0) for b in range(2)], 0)
    )
    scat_down = scatter_block(1)
    grad_pre = (dot(w_down, grad_rows, 0, 0) * slope[...]).astype(NARROW)
    put(3, dot(w_up, grad_pre, 0, 0))
    send(3, range(NX))
    mixed_up = dot(grad_pre, permuted, 1, 1).astype(NARROW)
    part[0] = chunked(
        jnp.concatenate([dot(mixed_up[N * b : N * b + N], pick_up[b], 1, 1) for b in range(2)], 0)
    )
    scat_up = scatter_block(0)
    def to_partner(i, value):
        halves[i] = value.reshape(2, half, tok)
        halves_out[i] = halves[i, 1 - core].astype(NARROW)
        copy = remote(halves_out.at[i], halves_in.at[i], half_send.at[i], half_recv.at[i], dp, partner)
        sends.append(copy)
        return copy

    def joined(i, base, copy):
        copy.wait_recv()
        return (
            base[core].astype(WIDE) + (halves[i, core] + halves_in[i].astype(WIDE))
        ).astype(NARROW)

    def plane_grad(s, q, block):
        value = dot(plane_rows(2 + s, q), block, 1, 1)
        if s == 1 and q in DIRECT:
            whole[q] = value.astype(NARROW)
            wholes[q, dp] = whole[q]
            return spread_out(
                lambda other: whole.at[q], lambda k: wholes.at[q, dp], qscat_send.at[s, q],
                qscat_recv.at[s, q],
            )
        qpart[s, q] = chunked(value)
        return scatter_plane(s, q)

    scat_second = [plane_grad(0, q, d_block) for q in range(2)]
    gath_down = gather_block(1, scat_down)
    scat_second += [plane_grad(0, q, d_block) for q in range(2, NX)]
    gath_up = gather_block(0, scat_up)
    out_half = to_partner(0, dot(ds_ref[...], got[2].reshape(rows, tok), 0, 0))
    scat_first = [plane_grad(1, 0, x_block), plane_grad(1, 1, x_block)]
    gath_second = [gather_plane(0, q, scat_second[q]) for q in range(NX)]
    scat_first += [plane_grad(1, q, x_block) for q in range(2, NX)]
    grad_half = to_partner(1, dot(uf_ref[...], got[3].reshape(rows, tok), 0, 0))
    mixed_ref[...] = joined(0, xb, out_half)
    gath_first = [None if q in DIRECT else gather_plane(1, q, scat_first[q]) for q in range(NX)]
    gtok_ref[...] = joined(1, db, grad_half)

    for j, copies in ((0, gath_up), (1, gath_down)):
        for copy in copies:
            copy.wait_recv()
        grads_ref[1 + j] = every[j].reshape(NX, 2 * plane, N)
    for s, j, found in ((0, 3, gath_second), (1, 0, gath_first)):
        for q in range(NX):
            for copy in found[q] or scat_first[q]:
                copy.wait_recv()
            if found[q]:
                grads_ref[j, plane_of(q)] = qevery[s, q].reshape(2 * plane, N)
            else:
                value = wholes[q, 0].astype(WIDE)
                for k in range(1, n_dp):
                    value = value + wholes[q, k].astype(WIDE)
                grads_ref[j, plane_of(q)] = value.astype(NARROW)

    for copy in sends:
        copy.wait_send()
    for i in range(4):
        landed(i, N - 1, send_sem.at[i]).wait()


def finish(scale, mixed_in, gtok_in, grads_in, mixed_ref, gtok_ref, uf_ref, us_ref, df_ref, ds_ref):
    mixed_ref[...] = mixed_in[...]
    gtok_ref[...] = gtok_in[...]
    for j, ref in enumerate((uf_ref, us_ref, df_ref, ds_ref)):
        ref[...] = (grads_in[j].astype(WIDE) * scale).reshape(ref.shape)


def shards(tokens, cotangent, up_first, up_second, down_first, down_second, perm_up, perm_down):
    half, tok = tokens.shape
    block = up_first.shape[2]
    rows = 2 * N
    n_dp = lax.axis_size("dp")
    vmem = pl.BlockSpec(memory_space=pltpu.VMEM)
    regular = pltpu.SemaphoreType.REGULAR
    dma = pltpu.SemaphoreType.DMA
    small = jax.ShapeDtypeStruct((half, tok), NARROW)
    some = rows // n_dp
    few = some // NX
    mixed, gtok, grads = pl.pallas_call(
        exchange,
        name="exchange",
        out_shape=(
            pltpu.VMEM((half, tok), NARROW),
            pltpu.VMEM((half, tok), NARROW),
            pltpu.VMEM((4, NX, rows // NX, block), NARROW),
        ),
        in_specs=[pl.BlockSpec(memory_space=pl.ANY)] * 8,
        out_specs=(vmem,) * 3,
        scratch_shapes=[
            pltpu.VMEM((2, half, tok), NARROW),
            pltpu.VMEM((2, half, tok), NARROW),
            pltpu.VMEM((rows, block), NARROW),
            pltpu.VMEM((2, block, block), NARROW),
            pltpu.VMEM((2, block, block), NARROW),
            pltpu.VMEM((rows, block), NARROW),
            pltpu.VMEM((1, N), jnp.int32),
            pltpu.VMEM((1, N), jnp.int32),
            pltpu.VMEM((4, N, 2, tok), NARROW),
            pltpu.VMEM((4, N, 2, tok), NARROW),
            pltpu.VMEM((rows, tok), NARROW),
            pltpu.VMEM((rows, tok), WIDE),
            pltpu.VMEM((2, 2, half, tok), WIDE),
            pltpu.VMEM((2, half, tok), NARROW),
            pltpu.VMEM((2, half, tok), NARROW),
            pltpu.VMEM((2, n_dp, some, block), NARROW),
            pltpu.VMEM((2, n_dp - 1, some, block), NARROW),
            pltpu.VMEM((2, some, block), NARROW),
            pltpu.VMEM((2, n_dp, some, block), NARROW),
            pltpu.VMEM((2, NX, n_dp, few, block), NARROW),
            pltpu.VMEM((2, NX, n_dp - 1, few, block), NARROW),
            pltpu.VMEM((2, NX, few, block), NARROW),
            pltpu.VMEM((2, NX, n_dp, few, block), NARROW),
            pltpu.VMEM((NX, rows // NX, block), NARROW),
            pltpu.VMEM((NX, n_dp, rows // NX, block), NARROW),
            regular,
            regular,
            regular,
            dma((8,)),
            dma((2,)),
            dma((2,)),
            dma((4,)),
            dma((4, NX)),
            dma((2,)),
            dma((2,)),
            *(dma((2, n_dp - 1)),) * 4,
            *(dma((2, NX, n_dp - 1)),) * 4,
        ],
        compiler_params=pltpu.CompilerParams(collective_id=0, has_side_effects=True),
    )(
        tokens, cotangent, up_first.reshape(rows, block), up_second, down_first,
        down_second.reshape(rows, block), perm_up.reshape(1, N), perm_down.reshape(1, N),
    )
    scale = 1.0 / math.sqrt(n_dp * tok)
    first = jax.ShapeDtypeStruct((1, rows, block), WIDE)
    second = jax.ShapeDtypeStruct((2, block, block), WIDE)
    return pl.pallas_call(
        functools.partial(finish, scale),
        name="finish",
        out_shape=(small, small, first, second, second, first),
        in_specs=[vmem] * 3,
        out_specs=(vmem,) * 6,
    )(*(pltpu.with_memory_space_constraint(v, pltpu.VMEM) for v in (mixed, gtok, grads)))


def solution(mesh):
    spread = P("loop", "dp")
    weight = P("loop", None, None)
    return jax.shard_map(
        shards,
        mesh=mesh,
        in_specs=(spread, spread, weight, weight, weight, weight, P(), P()),
        out_specs=(spread, spread, weight, weight, weight, weight),
        check_vma=False,
    )
```
